128 devices in a mesh: req: 64 (over z, y, x_hi, core), tp: 2 (over x_lo).
Axes of the slice: x: 4 (x_hi: 2, x_lo: 2; x = x_hi * 2 + x_lo), y: 4, z: 4, core: 2. Of those that a mesh axis runs over, the one named last changes fastest.
Arguments:
- arrivals: bfloat16 [32768, 2048], P('req', 'tp'), may hold values from -16 to 16
- packing: int32 [256], P('req'), may hold values from 0 to 255, as said below
- segment_ids: int32 [32768], P('req'), may hold values from 0 to 32767, as said below
- page_table: int32 [256], P('req'), may hold values from 0 to 255, as said below
- attn_gain: float32 [2048], replicated, may hold values from 0.25 to 1.75
- w_query: bfloat16 [2048, 2048], P(None, 'tp'), may hold values from -0.015625 to 0.015625
- w_key: bfloat16 [2048, 2048], P(None, 'tp'), may hold values from -0.125 to 0.125
- w_value: bfloat16 [2048, 2048], P(None, 'tp'), may hold values from -0.125 to 0.125
- w_out: bfloat16 [2048, 2048], P('tp'), may hold values from -0.1875 to 0.1875
- rel_bias: float32 [32, 32], P(None, 'tp'), may hold values from -4 to 260
- final_gain: float32 [2048], replicated, may hold values from 0.25 to 1.75
- cross_key: bfloat16 [2048, 2048], P(None, 'tp'), may hold values from -0.125 to 0.125
- cross_value: bfloat16 [2048, 2048], P(None, 'tp'), may hold values from -0.125 to 0.125
Outputs:
- hidden: bfloat16 [32768, 2048], P('req', 'tp')
- cache: bfloat16 [256, 128, 2, 2048], P('req', None, None, 'tp')
The draws below stay inside these ranges and needn't reach their ends.
Inputs may be any that keep to these rules, and one draw needn't show every extreme that they name: `packing`: A permutation of the block numbers; the entries of index r of req name, by their quotient by 4, the indices r XOR m for every m below 4, each exactly 1 times. `segment_ids`: Non-decreasing; every segment lies within the 512 tokens of one index of req and has at most 256 tokens; some index holds one of exactly 256. `page_table`: A permutation of the slots; the entries of index r of req name, by their quotient by 4, the indices r XOR m for every m below 4, each exactly 1 times; slot s lies on index s // 4 of req.
All inputs are finite; a program needn't handle non-finite values.
Results may differ from the reference program's by a relative error of at most 0.01.
Values may be sent and summed in bfloat16 or wider, within the bound.
No kernel may reach another device: no remote copies, remote signals or barrier semaphores. Data moves between devices by JAX's collectives and lax.ppermute only.
A program may use at most 256 MiB of HBM per device.

```python
import jax
import jax.numpy as jnp
from jax import lax

D = 2048
HEADS = 32
HEAD_DIM = 64
BUCKETS = 32
PAGE = 128
TOK_DEV = 512
INNER = 2048
HEAD_GROUPS = 2
LONG = 256
N_REQ = 64


def owner_slots(key_base, per_device, devices):
    group_size = min(per_device, devices)
    capacity = per_device // group_size
    key_a, key_b = jax.random.split(key_base, 2)
    lane_order = jax.vmap(lambda subkey: jax.random.permutation(subkey, per_device))(jax.random.split(key_a, devices)).astype(jnp.int32)
    arrangement = jax.vmap(lambda subkey: jax.random.permutation(subkey, per_device))(jax.random.split(key_b, devices)).astype(jnp.int32)
    sender = jnp.arange(devices, dtype=jnp.int32)[:, None]
    offset_bits = lane_order // capacity
    owners = jnp.bitwise_xor(sender, offset_bits).astype(jnp.int32)
    slots = owners * per_device + arrangement[owners, lane_order]
    return slots.reshape(-1).astype(jnp.int32)


def draw_packing(key, part):
    return owner_slots(jax.random.fold_in(key, 11), TOK_DEV // PAGE, N_REQ)


def draw_page_table(key, part):
    return owner_slots(jax.random.fold_in(key, 23), TOK_DEV // PAGE, N_REQ)


def draw_segment_ids(key, part):
    key_a, key_b = jax.random.split(jax.random.fold_in(key, 37))
    position = jnp.arange(TOK_DEV, dtype=jnp.int32)[None, :]
    device = jnp.arange(N_REQ, dtype=jnp.int32)[:, None]
    starts = jax.random.randint(key_a, (N_REQ, TOK_DEV), 0, 32) == 0
    starts = starts | (position % (LONG // 4) == 0)
    rotation = jax.random.randint(key_b, (), 0, 4)
    holder = (device + rotation) % 4 == 0
    starts = jnp.where(holder & (position < LONG), position == 0, starts)
    starts = starts | holder & (position == LONG)
    numbers = jnp.cumsum(starts.astype(jnp.int32), axis=1) - 1 + device * TOK_DEV
    return numbers.reshape(-1).astype(jnp.int32)


def draw_arrivals(key, part):
    key_a, key_b = jax.random.split(jax.random.fold_in(key, 41), 2)
    row_count = TOK_DEV * N_REQ
    column = jnp.arange(D, dtype=jnp.float32) / (D - 1)
    row_scale = 0.3 * 10.0 ** jax.random.uniform(key_b, (row_count, 1), jnp.float32, 0.0, 1.0)
    base = jnp.clip(jax.random.normal(key_a, (row_count, D), jnp.float32), -4.0, 4.0)
    column_scale = 3.0 ** (0.5 * column)
    return jnp.clip(base * row_scale * column_scale[None, :], -16.0, 16.0).astype(jnp.bfloat16)


def draw_rel_bias(key, part):
    key_a = jax.random.fold_in(jax.random.fold_in(key, 51), 0)
    return jnp.clip(jax.random.normal(key_a, (BUCKETS, HEADS), jnp.float32), -4.0, 4.0)


def raised(entries, own_key, source, target, blocks, factor):
    def block_of(axis_at):
        return (jnp.arange(entries.shape[axis_at]) // (entries.shape[axis_at] // blocks)).reshape((-1,) + (1,) * (entries.ndim - 1 - axis_at))

    near = jax.random.permutation(own_key, blocks)[block_of(target)]
    other_side = (block_of(target) + blocks // 2) % blocks
    return jnp.where((block_of(source) == near) | (block_of(source) == other_side), factor * entries, entries)


def levels(stream_key, shape, cuts, least, top_value):
    factor_of = 1.0
    for dim, shards_of in cuts:
        heights = jax.random.uniform(jax.random.fold_in(jax.random.fold_in(stream_key, 6), dim), (shards_of,), jnp.float32, least / len(cuts), top_value / len(cuts))
        factor_of = factor_of * jnp.repeat(jnp.exp(heights), shape[dim] // shards_of).reshape((-1,) + (1,) * (len(shape) - 1 - dim))
    return factor_of


def scatter_about(key, extent, spread, most, cuts=(), kind=jnp.bfloat16):
    result = spread * jax.random.normal(key, extent, jnp.float32)
    if cuts:
        result = result * levels(key, extent, cuts, -0.22, 0.18)
    return jnp.clip(result, -most, most).astype(kind)


def noise_with(own_key, extent, scale, most, cuts, heavy, kind=jnp.bfloat16):
    values = scale * jax.random.normal(own_key, extent, jnp.float32)
    if cuts:
        values = values * levels(own_key, extent, cuts, -0.22, 0.18)
    return jnp.clip(raised(values, jax.random.fold_in(own_key, 3), *heavy), -most, most).astype(kind)


def setup_inputs(seed: int = 0) -> dict:
    keys = jax.random.split(jax.random.key(seed), 14)
    return {
        "arrivals": draw_arrivals(jax.random.fold_in(keys[13], 71), 0),
        "packing": draw_packing(jax.random.fold_in(keys[13], 71), 0),
        "segment_ids": draw_segment_ids(jax.random.fold_in(keys[13], 71), 0),
        "page_table": draw_page_table(jax.random.fold_in(keys[13], 71), 0),
        "attn_gain": jnp.clip(1.0 + 0.15 * jax.random.normal(keys[4], (D,), jnp.float32), 0.25, 1.75),
        "w_query": scatter_about(keys[5], (D, INNER), (D * HEAD_DIM) ** -0.5, 0.015625, ((1, 2),)),
        "w_key": scatter_about(keys[6], (D, INNER), D ** -0.5, 0.125, ((1, 2),)),
        "w_value": scatter_about(keys[7], (D, INNER), D ** -0.5, 0.125, ((1, 2),)),
        "w_out": noise_with(keys[8], (INNER, D), INNER ** -0.5, 0.1875, ((0, 2),), (0, 1, 2, 2.0)),
        "rel_bias": draw_rel_bias(jax.random.fold_in(keys[13], 71), 0),
        "final_gain": jnp.clip(1.0 + 0.15 * jax.random.normal(keys[10], (D,), jnp.float32), 0.25, 1.75),
        "cross_key": scatter_about(keys[11], (D, INNER), D ** -0.5, 0.125, ((1, 2),)),
        "cross_value": scatter_about(keys[12], (D, INNER), D ** -0.5, 0.125, ((1, 2),)),
    }


epsilon = 1e-06
far_steps = (12, 16, 23, 32, 46, 64, 91)

def buckets(offsets):
    distance = jnp.abs(offsets)
    far_bucket = 8 + sum(((distance >= threshold).astype(jnp.int32) for threshold in far_steps))
    bucket_ids = jnp.where(distance < 8, distance, far_bucket).astype(jnp.int32)
    return bucket_ids + jnp.where(offsets > 0, 16, 0).astype(jnp.int32)

def rms_scale(row_set, gain_row):
    values = row_set.astype(jnp.float32)
    mean_square = lax.optimization_barrier(jnp.mean(values * values, axis=-1, keepdims=True))
    return (values * lax.rsqrt(mean_square + epsilon) * gain_row).astype(jnp.bfloat16)

def attend(queries, keys_local, values_local, segments, rel_bias):
    token_count = queries.shape[0]
    head_count = rel_bias.shape[1]
    head_dim = queries.shape[1] // head_count
    row_block = min(512, token_count)
    query_heads = queries.reshape(token_count, head_count, head_dim).astype(jnp.float32)
    key_heads = keys_local.reshape(token_count, head_count, head_dim).astype(jnp.float32)
    value_heads = values_local.reshape(token_count, head_count, head_dim).astype(jnp.float32)
    positions = jnp.arange(token_count, dtype=jnp.int32)
    bias_table = jnp.transpose(rel_bias)

    def one_block(first_row):
        row_queries = lax.dynamic_slice_in_dim(query_heads, first_row, row_block, 0)
        row_segments = lax.dynamic_slice_in_dim(segments, first_row, row_block, 0)
        scores = jnp.einsum('qhd,khd->hqk', row_queries, key_heads)
        row_positions = first_row + jnp.arange(row_block, dtype=jnp.int32)
        offsets = positions[None, :] - row_positions[:, None]
        bias_tile = jnp.take(bias_table, buckets(offsets), axis=1)
        same_segment = row_segments[:, None] == segments[None, :]
        scores = jnp.where(same_segment[None], scores + bias_tile, -jnp.inf)
        row_max = lax.optimization_barrier(jnp.max(scores, axis=-1, keepdims=True))
        weights = jnp.exp(scores - row_max)
        probabilities = (weights / lax.optimization_barrier(jnp.sum(weights, axis=-1, keepdims=True))).astype(jnp.bfloat16)
        mixed = jnp.einsum('hqk,khd->qhd', probabilities.astype(jnp.float32), value_heads)
        return mixed.astype(jnp.bfloat16)
    block_starts = (jnp.arange(token_count // row_block, dtype=jnp.int32) * row_block).astype(jnp.int32)
    outcome = lax.map(one_block, block_starts)
    return outcome.reshape(token_count, head_count * head_dim)

def reference(arrivals, packing, segment_ids, page_table, attn_gain, w_query, w_key, w_value, w_out, rel_bias, final_gain, cross_key, cross_value):
    token_count, width = arrivals.shape
    block_count = token_count // PAGE
    arrived = arrivals.reshape(block_count, PAGE, width)
    packed = jnp.zeros_like(arrived).at[packing].set(arrived).reshape(token_count, width)
    normed = rms_scale(packed, attn_gain)
    queries = jnp.dot(normed, w_query, preferred_element_type=jnp.float32).astype(jnp.bfloat16)
    keys_all = jnp.dot(normed, w_key, preferred_element_type=jnp.float32).astype(jnp.bfloat16)
    values_all = jnp.dot(normed, w_value, preferred_element_type=jnp.float32).astype(jnp.bfloat16)
    inner_width = w_query.shape[1]

    def per_device(pieces):
        return attend(pieces[0], pieces[1], pieces[2], pieces[3], rel_bias)
    context = lax.map(per_device, (queries.reshape(N_REQ, TOK_DEV, inner_width), keys_all.reshape(N_REQ, TOK_DEV, inner_width), values_all.reshape(N_REQ, TOK_DEV, inner_width), segment_ids.reshape(N_REQ, TOK_DEV))).reshape(token_count, inner_width)
    group_width = inner_width // HEAD_GROUPS

    def add_group(summed, group_index):
        context_group = lax.dynamic_slice_in_dim(context, group_index * group_width, group_width, 1)
        weight_group = lax.dynamic_slice_in_dim(w_out, group_index * group_width, group_width, 0)
        product = jnp.dot(context_group, weight_group, preferred_element_type=jnp.float32).astype(jnp.bfloat16)
        return (summed + lax.optimization_barrier(product).astype(jnp.float32), None)
    attended, unused_rest = lax.scan(add_group, jnp.zeros((token_count, width), jnp.float32), jnp.arange(HEAD_GROUPS, dtype=jnp.int32))
    hidden = (packed.astype(jnp.float32) + attended).astype(jnp.bfloat16)
    final = rms_scale(hidden, final_gain)
    cross_keys = jnp.dot(final, cross_key, preferred_element_type=jnp.float32).astype(jnp.bfloat16)
    cross_values = jnp.dot(final, cross_value, preferred_element_type=jnp.float32).astype(jnp.bfloat16)
    pages = jnp.stack([cross_keys, cross_values], axis=1).reshape(block_count, PAGE, 2, inner_width)
    cache = jnp.zeros_like(pages).at[page_table].set(pages)
    return (hidden, cache)
```

```python
import jax
import jax.numpy as jnp
from jax import lax
from jax.experimental import pallas as pl
from jax.experimental.pallas import tpu as pltpu
from jax.sharding import PartitionSpec as P

PAGE = 128
HEAD_DIM = 64
SPREAD = 384
GROUP = 256
MIB = 1 << 20

epsilon = 1e-06
far_steps = (12, 16, 23, 32, 46, 64, 91)
NEG = float("-inf")


def exchange(block, mask, flip):
    count = lax.axis_size("req")
    pairs = [(r * 2 + t, (r ^ mask) * 2 + (t ^ flip)) for r in range(count) for t in range(2)]
    return lax.ppermute(block, ("req", "tp"), pairs)


def buckets(offsets):
    distance = jnp.abs(offsets)
    far_bucket = 8 + sum((distance >= threshold).astype(jnp.int32) for threshold in far_steps)
    bucket_ids = jnp.where(distance < 8, distance, far_bucket)
    return bucket_ids + jnp.where(offsets > 0, 16, 0).astype(jnp.int32)


def any_spec():
    return pl.BlockSpec(memory_space=pl.ANY)


def smem_spec():
    return pl.BlockSpec(memory_space=pltpu.SMEM)


def params(mib, grid_rank=1):
    return pltpu.CompilerParams(
        dimension_semantics=("arbitrary",) * grid_rank, vmem_limit_bytes=mib * MIB
    )


def lane_order(packing, page_table, arrived, me):
    def body(packing_ref, table_ref, me_ref, rows_ref, *rest):
        row_outs, tag_outs, page_out, sems = rest[:4], rest[4:8], rest[8], rest[9]
        me_here = me_ref[0]
        copies = []
        for m in range(4):
            source = jnp.int32(0)
            pack_slot = jnp.int32(0)
            page = jnp.int32(0)
            page_slot = jnp.int32(0)
            for j in range(4):
                hit = ((packing_ref[j] // 4) ^ me_here) == m
                source = jnp.where(hit, j, source)
                pack_slot = jnp.where(hit, packing_ref[j] % 4, pack_slot)
                owned = ((table_ref[j] // 4) ^ me_here) == m
                page = jnp.where(owned, j, page)
                page_slot = jnp.where(owned, table_ref[j] % 4, page_slot)
            tag_outs[m][0] = pack_slot
            tag_outs[m][1] = page_slot
            page_out[m] = page
            copy = pltpu.make_async_copy(rows_ref.at[source], row_outs[m], sems.at[m])
            copy.start()
            copies.append(copy)
        for copy in copies:
            copy.wait()

    shape = jax.ShapeDtypeStruct(arrived.shape[1:], arrived.dtype)
    outs = pl.pallas_call(
        body,
        grid_spec=pltpu.PrefetchScalarGridSpec(
            num_scalar_prefetch=3,
            grid=(),
            in_specs=[any_spec()],
            out_specs=[any_spec()] * 4 + [smem_spec()] * 5,
            scratch_shapes=[pltpu.SemaphoreType.DMA((4,))],
        ),
        out_shape=[shape] * 4
        + [jax.ShapeDtypeStruct((2,), jnp.int32)] * 4
        + [jax.ShapeDtypeStruct((4,), jnp.int32)],
        name="lane_order",
    )(packing, page_table, me, arrived)
    return outs[:4], outs[4:8], outs[8]


def bias_tiles(rel_bias):
    table = jnp.transpose(rel_bias)
    heads = table.shape[0]

    def body(table_ref, out_ref):
        lane = lax.broadcasted_iota(jnp.int32, (heads, 512), 1)
        bucket_ids = buckets(jnp.where(lane < SPREAD, lane - PAGE, lane - PAGE - 512))
        values = table_ref[...]
        row = jnp.zeros((heads, 512), jnp.float32)
        for b in range(table.shape[1]):
            row = jnp.where(bucket_ids == b, values[:, b : b + 1], row)
        for h in range(heads):
            wide = jnp.broadcast_to(row[h : h + 1, :], (PAGE, 512))
            turned = pltpu.roll(wide, 0, 1, stride=1, stride_axis=0)
            out_ref[h * PAGE : (h + 1) * PAGE, :] = turned[:, :SPREAD]

    return pl.pallas_call(
        body,
        out_shape=jax.ShapeDtypeStruct((heads * PAGE, SPREAD), jnp.float32),
        compiler_params=pltpu.CompilerParams(vmem_limit_bytes=16 * MIB),
        name="bias_tiles",
    )(table)


def normalize(side, first_refs, second_refs, gain_ref, out_ref):
    half = first_refs[0].shape[-1]
    for i, (first_ref, second_ref) in enumerate(zip(first_refs, second_refs)):
        first = first_ref[...].astype(jnp.float32)
        second = second_ref[...].astype(jnp.float32)
        total = jnp.sum(first * first, axis=-1, keepdims=True) + jnp.sum(
            second * second, axis=-1, keepdims=True
        )
        scale = lax.rsqrt(total * (1.0 / (2 * half)) + epsilon)
        left = jnp.where(side == 0, first, second)
        right = jnp.where(side == 0, second, first)
        rows = slice(i * PAGE, (i + 1) * PAGE)
        out_ref[rows, :half] = (left * scale * gain_ref[:, :half]).astype(jnp.bfloat16)
        out_ref[rows, half:] = (right * scale * gain_ref[:, half:]).astype(jnp.bfloat16)


def project(part, first, second, side, gain, weights, earlier):
    half = first[0].shape[1]
    columns = weights[0].shape[1]
    steps = columns // GROUP

    def body(side_ref, f0, f1, s0, s1, gain_ref, wq, wk, wv, *rest):
        q_out, k_out, v_out, own_out, normed = rest[-5:]

        @pl.when(pl.program_id(0) == 0)
        def _():
            normalize(side_ref[0], (f0, f1), (s0, s1), gain_ref, normed)
            own_out[0] = f0[...]
            own_out[1] = f1[...]

        rows = normed[...]
        for w_ref, out in ((wq, q_out), (wk, k_out), (wv, v_out)):
            product = jnp.dot(rows, w_ref[...], preferred_element_type=jnp.float32)
            out[...] = product.astype(jnp.bfloat16).reshape(2, PAGE, GROUP)

    block = pl.BlockSpec((PAGE, half), lambda n, s: (0, 0))
    weight = pl.BlockSpec((2 * half, GROUP), lambda n, s: (0, n))
    out = pl.BlockSpec((2, PAGE, GROUP), lambda n, s: (part, 0, n))
    own = pl.BlockSpec((2, PAGE, half), lambda n, s: (part, 0, 0))
    shape = jax.ShapeDtypeStruct((4, PAGE, columns), jnp.bfloat16)
    return pl.pallas_call(
        body,
        grid_spec=pltpu.PrefetchScalarGridSpec(
            num_scalar_prefetch=1,
            grid=(steps,),
            in_specs=[block] * 4
            + [pl.BlockSpec((1, 2 * half), lambda n, s: (0, 0))]
            + [weight] * 3
            + [any_spec()] * len(earlier),
            out_specs=[out, out, out, own],
            scratch_shapes=[pltpu.VMEM((2 * PAGE, 2 * half), jnp.bfloat16)],
        ),
        out_shape=[shape, shape, shape, jax.ShapeDtypeStruct((4, PAGE, half), jnp.bfloat16)],
        input_output_aliases={9 + i: i for i in range(len(earlier))},
        compiler_params=params(24),
        cost_estimate=pl.CostEstimate(
            flops=2 * 2 * PAGE * 2 * half * 3 * columns,
            transcendentals=0,
            bytes_accessed=3 * 2 * half * columns * 2,
        ),
        name="project",
    )(side, *first, *second, gain, *weights, *earlier)


def lane_of(meta, block):
    lane = jnp.int32(0)
    for m in range(1, 4):
        lane = jnp.where(meta[2 * m] == block, m, lane)
    return lane


def attend(lanes, meta, segments, side, queries, keys_local, values_local, w_out, bias):
    inner = w_out.shape[0]
    width = w_out.shape[1]
    steps = inner // GROUP
    pair = 2 * HEAD_DIM

    def body(meta_ref, seg_ref, side_ref, q_ref, k_ref, v_ref, rows_ref, w_ref, bias_ref,
             own_out, send_out, total, ctx, m_sc, l_sc, a_sc, seg_sc):
        step = pl.program_id(0)

        @pl.when(step == 0)
        def _():
            total[...] = jnp.zeros_like(total)
            for i, m in enumerate(lanes):
                row = rows_ref[pl.ds(meta_ref[8 + m], 1), :]
                seg_sc[i] = jnp.transpose(jnp.broadcast_to(row, (PAGE, PAGE)))

        lane = lax.broadcasted_iota(jnp.int32, (PAGE, pair), 1)
        low = lane < HEAD_DIM
        ones = jnp.ones((PAGE, PAGE), jnp.bfloat16)
        for i, m in enumerate(lanes):
            block = meta_ref[8 + m]
            at = lane_of(meta_ref, block)

            def scores(key_block, key_at, delta, hp):
                cols = slice(hp * pair, (hp + 1) * pair)
                q = q_ref[at, :, cols]
                zero = jnp.zeros_like(q)
                stacked = jnp.concatenate([jnp.where(low, q, zero), jnp.where(low, zero, q)], axis=0)
                s = lax.dot_general(
                    stacked, k_ref[key_at, :, cols], (((1,), (1,)), ((), ())),
                    preferred_element_type=jnp.float32,
                )
                rows = slice(hp * 2 * PAGE, (hp + 1) * 2 * PAGE)
                if delta == 2:
                    s = s + bias_ref[rows, SPREAD - 1 : SPREAD]
                elif delta == -2:
                    s = s + bias_ref[rows, 0:1]
                else:
                    s = s + bias_ref[rows, (delta + 1) * PAGE : (delta + 2) * PAGE]
                same = seg_sc[i] == rows_ref[pl.ds(key_block, 1), :]
                hide = jnp.where(same, 0.0, NEG).astype(jnp.float32)
                return s + jnp.concatenate([hide, hide], axis=0)

            for hp in range(GROUP // pair):
                s = scores(block, at, 0, hp)
                top = jnp.max(s, axis=-1, keepdims=True)
                weights = jnp.exp(s - top).astype(jnp.bfloat16)
                m_sc[hp] = jnp.broadcast_to(top, (2 * PAGE, PAGE))
                l_sc[hp] = jnp.dot(weights, ones, preferred_element_type=jnp.float32)
                a_sc[hp] = jnp.dot(
                    weights, v_ref[at, :, hp * pair : (hp + 1) * pair],
                    preferred_element_type=jnp.float32,
                )

            for delta in (-1, 1, -2, 2):
                key_block = block + delta
                inside = jnp.logical_and(key_block >= 0, key_block < 4)
                if delta > 0:
                    last = block * PAGE + PAGE - 1
                    first = key_block * PAGE
                else:
                    last = key_block * PAGE + PAGE - 1
                    first = block * PAGE
                top_index = 4 * PAGE - 1
                joined = seg_ref[jnp.clip(last, 0, top_index)] == seg_ref[jnp.clip(first, 0, top_index)]

                @pl.when(jnp.logical_and(inside, joined))
                def _(key_block=key_block, delta=delta):
                    key_at = lane_of(meta_ref, key_block)
                    for hp in range(GROUP // pair):
                        s = scores(key_block, key_at, delta, hp)
                        before = m_sc[hp]
                        top = jnp.maximum(before, jnp.max(s, axis=-1, keepdims=True))
                        fade = jnp.exp(before - top)
                        weights = jnp.exp(s - top).astype(jnp.bfloat16)
                        m_sc[hp] = top
                        l_sc[hp] = l_sc[hp] * fade + jnp.dot(
                            weights, ones, preferred_element_type=jnp.float32
                        )
                        a_sc[hp] = a_sc[hp] * fade + jnp.dot(
                            weights, v_ref[key_at, :, hp * pair : (hp + 1) * pair],
                            preferred_element_type=jnp.float32,
                        )

            for hp in range(GROUP // pair):
                mixed = a_sc[hp] / l_sc[hp]
                ctx[i * PAGE : (i + 1) * PAGE, hp * pair : (hp + 1) * pair] = jnp.where(
                    low, mixed[:PAGE], mixed[PAGE:]
                ).astype(jnp.bfloat16)

        total[...] += jnp.dot(ctx[...], w_ref[...], preferred_element_type=jnp.float32)

        @pl.when(step == steps - 1)
        def _():
            half = width // 2
            left = total[:, :half].astype(jnp.bfloat16)
            right = total[:, half:].astype(jnp.bfloat16)
            own_out[...] = jnp.where(side_ref[0] == 0, left, right)
            send_out[...] = jnp.where(side_ref[0] == 0, right, left)

    heads = pl.BlockSpec((4, PAGE, GROUP), lambda g, *_: (0, 0, g))
    out = pl.BlockSpec((2 * PAGE, width // 2), lambda g, *_: (0, 0))
    shape = jax.ShapeDtypeStruct((2 * PAGE, width // 2), jnp.bfloat16)
    rows = GROUP // HEAD_DIM * PAGE
    pairs = GROUP // pair
    return pl.pallas_call(
        body,
        grid_spec=pltpu.PrefetchScalarGridSpec(
            num_scalar_prefetch=3,
            grid=(steps,),
            in_specs=[
                heads,
                heads,
                heads,
                pl.BlockSpec((4, PAGE), lambda g, *_: (0, 0)),
                pl.BlockSpec((GROUP, width), lambda g, *_: (g, 0)),
                pl.BlockSpec((rows, SPREAD), lambda g, *_: (g, 0)),
            ],
            out_specs=[out, out],
            scratch_shapes=[
                pltpu.VMEM((2 * PAGE, width), jnp.float32),
                pltpu.VMEM((2 * PAGE, GROUP), jnp.bfloat16),
                pltpu.VMEM((pairs, 2 * PAGE, PAGE), jnp.float32),
                pltpu.VMEM((pairs, 2 * PAGE, PAGE), jnp.float32),
                pltpu.VMEM((pairs, 2 * PAGE, pair), jnp.float32),
                pltpu.VMEM((2, PAGE, PAGE), jnp.int32),
            ],
        ),
        out_shape=[shape, shape],
        compiler_params=params(24),
        cost_estimate=pl.CostEstimate(
            flops=2 * 2 * PAGE * inner * width * 2,
            transcendentals=2 * PAGE * 512 * 16,
            bytes_accessed=inner * width * 2 + 10 * MIB,
        ),
        name="attend",
    )(meta, segments, side, queries, keys_local, values_local,
      segments.reshape(4, PAGE), w_out, bias)


def residual(lanes, meta, own, received, packed, earlier):
    half = own.shape[1]

    def page(i, meta_ref):
        return jnp.where(i == 0, meta_ref[8 + lanes[0]], meta_ref[8 + lanes[1]])

    def body(meta_ref, own_ref, got_ref, packed_ref, *rest):
        out, first, second = rest[-3:]
        added = own_ref[...].astype(jnp.float32) + got_ref[...].astype(jnp.float32)
        value = (packed_ref[0].astype(jnp.float32) + added).astype(jnp.bfloat16)
        out[0] = value

        @pl.when(pl.program_id(0) == 0)
        def _():
            first[...] = value

        @pl.when(pl.program_id(0) == 1)
        def _():
            second[...] = value

    block = pl.BlockSpec((PAGE, half), lambda i, s: (i, 0))
    alone = pl.BlockSpec((PAGE, half), lambda i, s: (0, 0))
    shape = jax.ShapeDtypeStruct((PAGE, half), jnp.bfloat16)
    return pl.pallas_call(
        body,
        grid_spec=pltpu.PrefetchScalarGridSpec(
            num_scalar_prefetch=1,
            grid=(2,),
            in_specs=[
                block,
                block,
                pl.BlockSpec((1, PAGE, half), lambda i, s: (lane_of(s, page(i, s)), 0, 0)),
            ]
            + [any_spec()] * len(earlier),
            out_specs=[pl.BlockSpec((1, PAGE, half), lambda i, s: (page(i, s), 0, 0)), alone, alone],
        ),
        out_shape=[jax.ShapeDtypeStruct((4, PAGE, half), jnp.bfloat16), shape, shape],
        input_output_aliases={4 + i: i for i in range(len(earlier))},
        compiler_params=params(8),
        name="residual",
    )(meta, own, received, packed, *earlier)


def cross(lanes, meta, side, first, second, gain, cross_key, cross_value, earlier):
    half = first[0].shape[1]
    columns = cross_key.shape[1]
    steps = columns // GROUP

    def body(meta_ref, side_ref, f0, f1, s0, s1, gain_ref, wk, wv, *rest):
        out, final, pages, sems = rest[-4:]
        step = pl.program_id(0)

        @pl.when(step == 0)
        def _():
            normalize(side_ref[0], (f0, f1), (s0, s1), gain_ref, final)

        rows = final[...]
        keys_part = jnp.dot(rows, wk[...], preferred_element_type=jnp.float32).astype(jnp.bfloat16)
        values_part = jnp.dot(rows, wv[...], preferred_element_type=jnp.float32).astype(jnp.bfloat16)
        both = jnp.stack([keys_part, values_part], axis=1)
        here = pl.ds(pl.multiple_of(step * GROUP, GROUP), GROUP)
        pages[0, :, :, here] = both[:PAGE]
        pages[1, :, :, here] = both[PAGE:]

        @pl.when(step == steps - 1)
        def _():
            copies = [
                pltpu.make_async_copy(pages.at[i], out.at[meta_ref[2 * m + 1]], sems.at[i])
                for i, m in enumerate(lanes)
            ]
            for copy in copies:
                copy.start()
            for copy in copies:
                copy.wait()

    block = pl.BlockSpec((PAGE, half), lambda n, *_: (0, 0))
    weight = pl.BlockSpec((2 * half, GROUP), lambda n, *_: (0, n))
    return pl.pallas_call(
        body,
        grid_spec=pltpu.PrefetchScalarGridSpec(
            num_scalar_prefetch=2,
            grid=(steps,),
            in_specs=[block] * 4
            + [pl.BlockSpec((1, 2 * half), lambda n, *_: (0, 0)), weight, weight]
            + [any_spec()] * len(earlier),
            out_specs=any_spec(),
            scratch_shapes=[
                pltpu.VMEM((2 * PAGE, 2 * half), jnp.bfloat16),
                pltpu.VMEM((2, PAGE, 2, columns), jnp.bfloat16),
                pltpu.SemaphoreType.DMA((2,)),
            ],
        ),
        out_shape=jax.ShapeDtypeStruct((4, PAGE, 2, columns), jnp.bfloat16),
        input_output_aliases={9: 0} if earlier else {},
        compiler_params=params(24),
        cost_estimate=pl.CostEstimate(
            flops=2 * 2 * PAGE * 2 * half * 2 * columns,
            transcendentals=0,
            bytes_accessed=2 * 2 * half * columns * 2,
        ),
        name="cross",
    )(meta, side, *first, *second, gain, cross_key, cross_value, *earlier)


def near(rows):
    other_zero = exchange(rows[0], 0, 1)
    own_one = exchange(rows[1], 1, 0)
    other_one = exchange(rows[1], 1, 1)
    return (rows[0], own_one), (other_zero, other_one)


def far(rows):
    other_two = exchange(rows[0], 2, 1)
    other_three = exchange(rows[1], 3, 1)
    own_two = exchange(other_two, 0, 1)
    own_three = exchange(other_three, 0, 1)
    return (own_two, own_three), (other_two, other_three)


def shards(
    arrivals,
    packing,
    segment_ids,
    page_table,
    attn_gain,
    w_query,
    w_key,
    w_value,
    w_out,
    rel_bias,
    final_gain,
    cross_key,
    cross_value,
):
    token_count, half = arrivals.shape
    me = lax.axis_index("req").astype(jnp.int32).reshape(1)
    side = lax.axis_index("tp").astype(jnp.int32).reshape(1)
    rows, tags, pages = lane_order(packing, page_table, arrivals.reshape(4, PAGE, half), me)
    far_own, far_other = far(rows[2:])
    near_own, near_other = near(rows[:2])
    meta = jnp.concatenate([tags[0]] + [exchange(tags[m], m, 0) for m in (1, 2, 3)] + [pages])
    bias = bias_tiles(rel_bias)
    attn_row = attn_gain.reshape(1, 2 * half)
    final_row = final_gain.reshape(1, 2 * half)
    weights = (w_query, w_key, w_value)
    held = project(0, near_own, near_other, side, attn_row, weights, ())
    queries, keys_local, values_local, packed = project(
        1, far_own, far_other, side, attn_row, weights, tuple(held)
    )
    own_far, send_far = attend(
        (2, 3), meta, segment_ids, side, queries, keys_local, values_local, w_out, bias
    )
    got_far = exchange(send_far, 0, 1)
    own_near, send_near = attend(
        (0, 1), meta, segment_ids, side, queries, keys_local, values_local, w_out, bias
    )
    got_near = exchange(send_near, 0, 1)
    hidden, hidden_two, hidden_three = residual((2, 3), meta, own_far, got_far, packed, ())
    far_first, far_second = far((hidden_two, hidden_three))
    hidden, hidden_zero, hidden_one = residual((0, 1), meta, own_near, got_near, packed, (hidden,))
    near_first, near_second = near((hidden_zero, hidden_one))
    cache = cross(
        (0, 1), meta, side, near_first, near_second, final_row, cross_key, cross_value, ()
    )
    cache = cross(
        (2, 3), meta, side, far_first, far_second, final_row, cross_key, cross_value, (cache,)
    )
    return (hidden.reshape(token_count, half), cache)


def solution(mesh):
    return jax.shard_map(
        shards,
        mesh=mesh,
        in_specs=(
            P("req", "tp"),
            P("req"),
            P("req"),
            P("req"),
            P(),
            P(None, "tp"),
            P(None, "tp"),
            P(None, "tp"),
            P("tp", None),
            P(None, "tp"),
            P(),
            P(None, "tp"),
            P(None, "tp"),
        ),
        out_specs=(P("req", "tp"), P("req", None, None, "tp")),
        check_vma=False,
    )
```

```python
import jax
import jax.numpy as jnp
from jax import lax
from jax.experimental import pallas as pl
from jax.experimental.pallas import tpu as pltpu
from jax.sharding import PartitionSpec as P

PAGE = 128
HEAD_DIM = 64
SPREAD = 640
TURN = 1024
GROUP = 256
MIB = 1 << 20

epsilon = 1e-06
far_steps = (12, 16, 23, 32, 46, 64, 91)
NEG = float("-inf")


def exchange(block, mask, flip):
    count = lax.axis_size("req")
    pairs = [(r * 2 + t, (r ^ mask) * 2 + (t ^ flip)) for r in range(count) for t in range(2)]
    return lax.ppermute(block, ("req", "tp"), pairs)


def buckets(offsets):
    distance = jnp.abs(offsets)
    far_bucket = 8 + sum((distance >= threshold).astype(jnp.int32) for threshold in far_steps)
    bucket_ids = jnp.where(distance < 8, distance, far_bucket)
    return bucket_ids + jnp.where(offsets > 0, 16, 0).astype(jnp.int32)


def any_spec():
    return pl.BlockSpec(memory_space=pl.ANY)


def smem_spec():
    return pl.BlockSpec(memory_space=pltpu.SMEM)


def hbm_spec():
    return pl.BlockSpec(memory_space=pltpu.HBM)


def vmem_spec():
    return pl.BlockSpec(memory_space=pltpu.VMEM)


def params(mib, grid_rank=1):
    return pltpu.CompilerParams(
        dimension_semantics=("arbitrary",) * grid_rank, vmem_limit_bytes=mib * MIB
    )


def lane_order(packing, page_table, arrived, me):
    def body(packing_ref, table_ref, me_ref, rows_ref, *rest):
        row_outs, tag_outs, page_out = rest[:4], rest[4:8], rest[8]
        me_here = me_ref[0]
        for m in range(4):
            source = jnp.int32(0)
            pack_slot = jnp.int32(0)
            page = jnp.int32(0)
            page_slot = jnp.int32(0)
            for j in range(4):
                hit = ((packing_ref[j] // 4) ^ me_here) == m
                source = jnp.where(hit, j, source)
                pack_slot = jnp.where(hit, packing_ref[j] % 4, pack_slot)
                owned = ((table_ref[j] // 4) ^ me_here) == m
                page = jnp.where(owned, j, page)
                page_slot = jnp.where(owned, table_ref[j] % 4, page_slot)
            tag_outs[m][0] = pack_slot
            tag_outs[m][1] = page_slot
            page_out[m] = page
            row_outs[m][...] = rows_ref[source]

    shape = jax.ShapeDtypeStruct(arrived.shape[1:], arrived.dtype)
    outs = pl.pallas_call(
        body,
        grid_spec=pltpu.PrefetchScalarGridSpec(
            num_scalar_prefetch=3,
            grid=(),
            in_specs=[vmem_spec()],
            out_specs=[vmem_spec()] * 4 + [smem_spec()] * 5,
        ),
        out_shape=[shape] * 4
        + [jax.ShapeDtypeStruct((2,), jnp.int32)] * 4
        + [jax.ShapeDtypeStruct((4,), jnp.int32)],
        compiler_params=pltpu.CompilerParams(vmem_limit_bytes=8 * MIB),
        name="lane_order",
    )(packing, page_table, me, arrived)
    return outs[:4], outs[4:8], outs[8]


def bias_tiles(rel_bias):
    table = jnp.transpose(rel_bias)
    heads = table.shape[0]

    def body(table_ref, out_ref):
        lane = lax.broadcasted_iota(jnp.int32, (heads, TURN), 1)
        bucket_ids = buckets(jnp.where(lane < SPREAD, lane - 2 * PAGE, lane - 2 * PAGE - TURN))
        values = table_ref[...]
        row = jnp.zeros((heads, TURN), jnp.float32)
        for b in range(table.shape[1]):
            row = jnp.where(bucket_ids == b, values[:, b : b + 1], row)
        for h in range(heads):
            wide = jnp.broadcast_to(row[h : h + 1, :], (PAGE, TURN))
            turned = pltpu.roll(wide, 0, 1, stride=1, stride_axis=0)
            out_ref[h * PAGE : (h + 1) * PAGE, :] = turned[:, :SPREAD]

    return pl.pallas_call(
        body,
        out_shape=jax.ShapeDtypeStruct((heads * PAGE, SPREAD), jnp.float32),
        compiler_params=pltpu.CompilerParams(vmem_limit_bytes=16 * MIB),
        cost_estimate=pl.CostEstimate(flops=0, transcendentals=0, bytes_accessed=48 * MIB),
        name="bias_tiles",
    )(table)


def normalize(side, first_refs, second_refs, gain_ref, out_ref):
    half = first_refs[0].shape[-1]
    for i, (first_ref, second_ref) in enumerate(zip(first_refs, second_refs)):
        first = first_ref[...].astype(jnp.float32)
        second = second_ref[...].astype(jnp.float32)
        total = jnp.sum(first * first, axis=-1, keepdims=True) + jnp.sum(
            second * second, axis=-1, keepdims=True
        )
        scale = lax.rsqrt(total * (1.0 / (2 * half)) + epsilon)
        left = jnp.where(side == 0, first, second)
        right = jnp.where(side == 0, second, first)
        rows = slice(i * PAGE, (i + 1) * PAGE)
        out_ref[rows, :half] = (left * scale * gain_ref[:, :half]).astype(jnp.bfloat16)
        out_ref[rows, half:] = (right * scale * gain_ref[:, half:]).astype(jnp.bfloat16)


def project(part, first, second, side, gain, weights, earlier):
    half = first[0].shape[1]
    columns = weights[0].shape[1]

    starts = range(0, columns, GROUP)

    def body(side_ref, f0, f1, s0, s1, gain_ref, wq, wk, wv, *rest):
        q_out, k_out, v_out, own_out, normed, held, sems = rest[-7:]
        copies = []
        for n, start in enumerate(starts):
            here = slice(start, start + GROUP)
            for i, w_ref in enumerate((wq, wk, wv)):
                copy = pltpu.make_async_copy(w_ref.at[:, here], held.at[i, :, here], sems.at[n, i])
                copy.start()
                copies.append(copy)
        normalize(side_ref[0], (f0, f1), (s0, s1), gain_ref, normed)
        own_out[0] = f0[...]
        own_out[1] = f1[...]
        for n, start in enumerate(starts):
            here = slice(start, start + GROUP)
            for i, out in enumerate((q_out, k_out, v_out)):
                copies[3 * n + i].wait()
                product = jnp.dot(normed[...], held[i, :, here], preferred_element_type=jnp.float32)
                out[:, :, here] = product.astype(jnp.bfloat16).reshape(2, PAGE, GROUP)

    out = pl.BlockSpec((2, PAGE, columns), lambda n, s: (part, 0, 0))
    own = pl.BlockSpec((2, PAGE, half), lambda n, s: (part, 0, 0))
    shape = jax.ShapeDtypeStruct((4, PAGE, columns), jnp.bfloat16)
    return pl.pallas_call(
        body,
        grid_spec=pltpu.PrefetchScalarGridSpec(
            num_scalar_prefetch=1,
            grid=(1,),
            in_specs=[vmem_spec()] * 5 + [hbm_spec()] * 3 + [any_spec()] * len(earlier),
            out_specs=[out, out, out, own],
            scratch_shapes=[
                pltpu.VMEM((2 * PAGE, 2 * half), jnp.bfloat16),
                pltpu.VMEM((3, 2 * half, columns), jnp.bfloat16),
                pltpu.SemaphoreType.DMA((len(starts), 3)),
            ],
        ),
        out_shape=[shape, shape, shape, jax.ShapeDtypeStruct((4, PAGE, half), jnp.bfloat16)],
        input_output_aliases={9 + i: i for i in range(len(earlier))},
        compiler_params=params(24),
        cost_estimate=pl.CostEstimate(
            flops=2 * 2 * PAGE * 2 * half * 3 * columns,
            transcendentals=0,
            bytes_accessed=2 * 2 * half * columns,
        ),
        name="project",
    )(side, *first, *second, gain, *weights, *earlier)


def lane_of(meta, block):
    lane = jnp.int32(0)
    for m in range(1, 4):
        lane = jnp.where(meta[2 * m] == block, m, lane)
    return lane


def attend(lanes, meta, segments, side, queries, keys_local, values_local, w_out, bias):
    inner = w_out.shape[0]
    width = w_out.shape[1]
    pair = 2 * HEAD_DIM
    pairs = inner // pair
    tall = 2 * PAGE

    def body(meta_ref, seg_ref, side_ref, q_ref, k_ref, v_ref, rows_ref, w_ref, bias_ref,
             own_out, send_out, ctx, m_sc, a_sc, seg_sc):
        low = lax.broadcasted_iota(jnp.int32, (PAGE, pair), 1) < HEAD_DIM
        ones = jnp.ones((PAGE, PAGE), jnp.bfloat16)

        def hidden_pairs(i, key_block):
            same = seg_sc[i] == rows_ref[pl.ds(key_block, 1), :]
            return jnp.where(same, 0.0, NEG).astype(jnp.float32)

        def scores(at, key_at, hide, tile, p):
            cols = slice(p * pair, (p + 1) * pair)
            q = q_ref[at, :, cols]
            zero = jnp.zeros_like(q)
            stacked = jnp.concatenate([jnp.where(low, q, zero), jnp.where(low, zero, q)], axis=0)
            s = lax.dot_general(
                stacked, k_ref[key_at, :, cols], (((1,), (1,)), ((), ())),
                preferred_element_type=jnp.float32,
            )
            s = s + bias_ref[p * tall : (p + 1) * tall, tile]
            return s + jnp.concatenate([hide, hide], axis=0)

        def weighted(weights, key_at, p):
            wide = jnp.concatenate([v_ref[key_at, :, p * pair : (p + 1) * pair], ones], axis=1)
            return jnp.dot(weights, wide, preferred_element_type=jnp.float32)

        places = []
        for i, m in enumerate(lanes):
            block = meta_ref[8 + m]
            row = rows_ref[pl.ds(block, 1), :]
            seg_sc[i] = jnp.transpose(jnp.broadcast_to(row, (PAGE, PAGE)))
            places.append((block, lane_of(meta_ref, block)))
        for i, (block, at) in enumerate(places):
            hide = hidden_pairs(i, block)
            for p in range(pairs):
                s = scores(at, at, hide, slice(2 * PAGE, 3 * PAGE), p)
                top = jnp.max(s, axis=-1, keepdims=True)
                weights = jnp.exp(s - top).astype(jnp.bfloat16)
                m_sc[i, p] = jnp.broadcast_to(top, (tall, PAGE))
                a_sc[i, p] = weighted(weights, at, p)

        @pl.loop(0, 8)
        def _(turn):
            i = turn // 4
            slot = turn % 4
            delta = jnp.where(slot < 2, slot - 2, slot - 1)
            block = jnp.where(i == 0, places[0][0], places[1][0])
            at = jnp.where(i == 0, places[0][1], places[1][1])
            key_block = block + delta
            last = jnp.minimum(block, key_block) * PAGE + PAGE - 1
            first = jnp.maximum(block, key_block) * PAGE
            top_index = 4 * PAGE - 1
            joined = seg_ref[jnp.clip(last, 0, top_index)] == seg_ref[jnp.clip(first, 0, top_index)]
            inside = jnp.logical_and(key_block >= 0, key_block < 4)

            @pl.when(jnp.logical_and(inside, joined))
            def _():
                key_at = lane_of(meta_ref, key_block)
                hide = hidden_pairs(i, key_block)
                tile = pl.ds(pl.multiple_of((delta + 2) * PAGE, PAGE), PAGE)
                for p in range(pairs):
                    s = scores(at, key_at, hide, tile, p)
                    before = m_sc[i, p]
                    top = jnp.maximum(before, jnp.max(s, axis=-1, keepdims=True))
                    fade = jnp.exp(before - top)
                    weights = jnp.exp(s - top).astype(jnp.bfloat16)
                    m_sc[i, p] = top
                    a_sc[i, p] = a_sc[i, p] * jnp.concatenate([fade, fade], axis=1) + weighted(
                        weights, key_at, p
                    )

        for i in range(2):
            for p in range(pairs):
                mixed = jnp.where(low, a_sc[i, p, :PAGE, :pair], a_sc[i, p, PAGE:, :pair])
                total = jnp.where(low, a_sc[i, p, :PAGE, pair:], a_sc[i, p, PAGE:, pair:])
                ctx[i * PAGE : (i + 1) * PAGE, p * pair : (p + 1) * pair] = (mixed / total).astype(
                    jnp.bfloat16
                )

        half = width // 2
        for out, here in ((own_out, side_ref[0]), (send_out, 1 - side_ref[0])):
            for start in range(0, half, GROUP):
                at = pl.multiple_of(here * half + start, GROUP)
                out[:, start : start + GROUP] = jnp.dot(
                    ctx[...], w_ref[:, pl.ds(at, GROUP)], preferred_element_type=jnp.float32
                ).astype(jnp.bfloat16)

    shape = jax.ShapeDtypeStruct((tall, width // 2), jnp.bfloat16)
    return pl.pallas_call(
        body,
        grid_spec=pltpu.PrefetchScalarGridSpec(
            num_scalar_prefetch=3,
            grid=(1,),
            in_specs=[vmem_spec()] * 6,
            out_specs=[vmem_spec()] * 2,
            scratch_shapes=[
                pltpu.VMEM((tall, inner), jnp.bfloat16),
                pltpu.VMEM((2, pairs, tall, PAGE), jnp.float32),
                pltpu.VMEM((2, pairs, tall, pair + PAGE), jnp.float32),
                pltpu.VMEM((2, PAGE, PAGE), jnp.int32),
            ],
        ),
        out_shape=[shape, shape],
        compiler_params=params(24),
        cost_estimate=pl.CostEstimate(
            flops=2 * tall * inner * width * 2,
            transcendentals=tall * 512 * 16,
            bytes_accessed=10 * MIB,
        ),
        name="attend",
    )(meta, segments, side, queries, keys_local, values_local,
      segments.reshape(4, PAGE), w_out, bias)


def residual(lanes, meta, own, received, packed, earlier):
    half = own.shape[1]

    def page(i, meta_ref):
        return jnp.where(i == 0, meta_ref[8 + lanes[0]], meta_ref[8 + lanes[1]])

    def body(meta_ref, own_ref, got_ref, packed_ref, *rest):
        out, first, second = rest[-3:]
        added = own_ref[...].astype(jnp.float32) + got_ref[...].astype(jnp.float32)
        value = (packed_ref[0].astype(jnp.float32) + added).astype(jnp.bfloat16)
        out[0] = value

        @pl.when(pl.program_id(0) == 0)
        def _():
            first[...] = value

        @pl.when(pl.program_id(0) == 1)
        def _():
            second[...] = value

    block = pl.BlockSpec((PAGE, half), lambda i, s: (i, 0))
    alone = pl.BlockSpec((PAGE, half), lambda i, s: (0, 0))
    shape = jax.ShapeDtypeStruct((PAGE, half), jnp.bfloat16)
    return pl.pallas_call(
        body,
        grid_spec=pltpu.PrefetchScalarGridSpec(
            num_scalar_prefetch=1,
            grid=(2,),
            in_specs=[
                block,
                block,
                pl.BlockSpec((1, PAGE, half), lambda i, s: (lane_of(s, page(i, s)), 0, 0)),
            ]
            + [any_spec()] * len(earlier),
            out_specs=[pl.BlockSpec((1, PAGE, half), lambda i, s: (page(i, s), 0, 0)), alone, alone],
        ),
        out_shape=[jax.ShapeDtypeStruct((4, PAGE, half), jnp.bfloat16), shape, shape],
        input_output_aliases={4 + i: i for i in range(len(earlier))},
        compiler_params=params(8),
        name="residual",
    )(meta, own, received, packed, *earlier)


def cross(lanes, meta, side, first, second, gain, cross_key, cross_value, earlier):
    half = first[0].shape[1]
    columns = cross_key.shape[1]

    def body(meta_ref, side_ref, f0, f1, s0, s1, gain_ref, wk, wv, *rest):
        out, final, pages, sems = rest[-4:]
        normalize(side_ref[0], (f0, f1), (s0, s1), gain_ref, final)
        copies = []
        for start in range(0, columns, GROUP):
            here = slice(start, start + GROUP)
            keys_part, values_part = (
                jnp.dot(final[...], w_ref[:, here], preferred_element_type=jnp.float32).astype(jnp.bfloat16)
                for w_ref in (wk, wv)
            )
            both = jnp.stack([keys_part, values_part], axis=1)
            for i, m in enumerate(lanes):
                pages[i, :, :, here] = both[i * PAGE : (i + 1) * PAGE]
        for i, m in enumerate(lanes):
            copy = pltpu.make_async_copy(pages.at[i], out.at[meta_ref[2 * m + 1]], sems.at[i])
            copy.start()
            copies.append(copy)
        for copy in copies:
            copy.wait()

    return pl.pallas_call(
        body,
        grid_spec=pltpu.PrefetchScalarGridSpec(
            num_scalar_prefetch=2,
            grid=(1,),
            in_specs=[vmem_spec()] * 7 + [any_spec()] * len(earlier),
            out_specs=any_spec(),
            scratch_shapes=[
                pltpu.VMEM((2 * PAGE, 2 * half), jnp.bfloat16),
                pltpu.VMEM((2, PAGE, 2, columns), jnp.bfloat16),
                pltpu.SemaphoreType.DMA((2,)),
            ],
        ),
        out_shape=jax.ShapeDtypeStruct((4, PAGE, 2, columns), jnp.bfloat16),
        input_output_aliases={9: 0} if earlier else {},
        compiler_params=params(24),
        cost_estimate=pl.CostEstimate(
            flops=2 * 2 * PAGE * 2 * half * 2 * columns,
            transcendentals=0,
            bytes_accessed=2 * 2 * half * columns * 2,
        ),
        name="cross",
    )(meta, side, *first, *second, gain, cross_key, cross_value, *earlier)


def near(rows):
    other_zero = exchange(rows[0], 0, 1)
    own_one = exchange(rows[1], 1, 0)
    other_one = exchange(rows[1], 1, 1)
    return (rows[0], own_one), (other_zero, other_one)


def far(rows):
    other_two = exchange(rows[0], 2, 1)
    other_three = exchange(rows[1], 3, 1)
    own_two = exchange(other_two, 0, 1)
    own_three = exchange(other_three, 0, 1)
    return (own_two, own_three), (other_two, other_three)


def shards(
    arrivals,
    packing,
    segment_ids,
    page_table,
    attn_gain,
    w_query,
    w_key,
    w_value,
    w_out,
    rel_bias,
    final_gain,
    cross_key,
    cross_value,
):
    token_count, half = arrivals.shape
    me = lax.axis_index("req").astype(jnp.int32).reshape(1)
    side = lax.axis_index("tp").astype(jnp.int32).reshape(1)
    rows, tags, pages = lane_order(packing, page_table, arrivals.reshape(4, PAGE, half), me)
    far_own, far_other = far(rows[2:])
    near_own, near_other = near(rows[:2])
    meta = jnp.concatenate([tags[0]] + [exchange(tags[m], m, 0) for m in (1, 2, 3)] + [pages])
    bias = bias_tiles(rel_bias)
    attn_row = attn_gain.reshape(1, 2 * half)
    final_row = final_gain.reshape(1, 2 * half)
    weights = (w_query, w_key, w_value)
    held = project(0, near_own, near_other, side, attn_row, weights, ())
    queries, keys_local, values_local, packed = project(
        1, far_own, far_other, side, attn_row, weights, tuple(held)
    )
    own_far, send_far = attend(
        (2, 3), meta, segment_ids, side, queries, keys_local, values_local, w_out, bias
    )
    got_far = exchange(send_far, 0, 1)
    own_near, send_near = attend(
        (0, 1), meta, segment_ids, side, queries, keys_local, values_local, w_out, bias
    )
    got_near = exchange(send_near, 0, 1)
    hidden, hidden_two, hidden_three = residual((2, 3), meta, own_far, got_far, packed, ())
    far_first, far_second = far((hidden_two, hidden_three))
    hidden, hidden_zero, hidden_one = residual((0, 1), meta, own_near, got_near, packed, (hidden,))
    near_first, near_second = near((hidden_zero, hidden_one))
    cache = cross(
        (0, 1), meta, side, near_first, near_second, final_row, cross_key, cross_value, ()
    )
    cache = cross(
        (2, 3), meta, side, far_first, far_second, final_row, cross_key, cross_value, (cache,)
    )
    return (hidden.reshape(token_count, half), cache)


def solution(mesh):
    return jax.shard_map(
        shards,
        mesh=mesh,
        in_specs=(
            P("req", "tp"),
            P("req"),
            P("req"),
            P("req"),
            P(),
            P(None, "tp"),
            P(None, "tp"),
            P(None, "tp"),
            P("tp", None),
            P(None, "tp"),
            P(),
            P(None, "tp"),
            P(None, "tp"),
        ),
        out_specs=(P("req", "tp"), P("req", None, None, "tp")),
        check_vma=False,
    )
```

```python
import jax
import jax.numpy as jnp
from jax import lax
from jax.experimental import pallas as pl
from jax.experimental.pallas import tpu as pltpu
from jax.sharding import PartitionSpec as P

PAGE = 128
HEAD_DIM = 64
SPREAD = 640
TURN = 1024
GROUP = 256
MIB = 1 << 20

epsilon = 1e-06
far_steps = (12, 16, 23, 32, 46, 64, 91)
NEG = float("-inf")


def exchange(block, mask, flip):
    count = lax.axis_size("req")
    pairs = [(r * 2 + t, (r ^ mask) * 2 + (t ^ flip)) for r in range(count) for t in range(2)]
    return lax.ppermute(block, ("req", "tp"), pairs)


def buckets(offsets):
    distance = jnp.abs(offsets)
    far_bucket = 8 + sum((distance >= threshold).astype(jnp.int32) for threshold in far_steps)
    bucket_ids = jnp.where(distance < 8, distance, far_bucket)
    return bucket_ids + jnp.where(offsets > 0, 16, 0).astype(jnp.int32)


def any_spec():
    return pl.BlockSpec(memory_space=pl.ANY)


def smem_spec():
    return pl.BlockSpec(memory_space=pltpu.SMEM)


def hbm_spec():
    return pl.BlockSpec(memory_space=pltpu.HBM)


def vmem_spec():
    return pl.BlockSpec(memory_space=pltpu.VMEM)


def params(mib, grid_rank=1):
    return pltpu.CompilerParams(
        dimension_semantics=("arbitrary",) * grid_rank, vmem_limit_bytes=mib * MIB
    )


def lane_order(packing, page_table, arrived, me):
    def body(packing_ref, table_ref, me_ref, rows_ref, *rest):
        row_outs, tag_outs, page_out = rest[:4], rest[4:8], rest[8]
        me_here = me_ref[0]
        for m in range(4):
            source = jnp.int32(0)
            pack_slot = jnp.int32(0)
            page = jnp.int32(0)
            page_slot = jnp.int32(0)
            for j in range(4):
                hit = ((packing_ref[j] // 4) ^ me_here) == m
                source = jnp.where(hit, j, source)
                pack_slot = jnp.where(hit, packing_ref[j] % 4, pack_slot)
                owned = ((table_ref[j] // 4) ^ me_here) == m
                page = jnp.where(owned, j, page)
                page_slot = jnp.where(owned, table_ref[j] % 4, page_slot)
            tag_outs[m][0] = pack_slot
            tag_outs[m][1] = page_slot
            page_out[m] = page
            row_outs[m][...] = rows_ref[source]

    shape = jax.ShapeDtypeStruct(arrived.shape[1:], arrived.dtype)
    outs = pl.pallas_call(
        body,
        grid_spec=pltpu.PrefetchScalarGridSpec(
            num_scalar_prefetch=3,
            grid=(),
            in_specs=[vmem_spec()],
            out_specs=[vmem_spec()] * 4 + [smem_spec()] * 5,
        ),
        out_shape=[shape] * 4
        + [jax.ShapeDtypeStruct((2,), jnp.int32)] * 4
        + [jax.ShapeDtypeStruct((4,), jnp.int32)],
        compiler_params=pltpu.CompilerParams(vmem_limit_bytes=8 * MIB),
        name="lane_order",
    )(packing, page_table, me, arrived)
    return outs[:4], outs[4:8], outs[8]


def bias_tiles(rel_bias):
    table = jnp.transpose(rel_bias)
    heads = table.shape[0]

    def body(table_ref, out_ref):
        lane = lax.broadcasted_iota(jnp.int32, (heads, TURN), 1)
        bucket_ids = buckets(jnp.where(lane < SPREAD, lane - 2 * PAGE, lane - 2 * PAGE - TURN))
        values = table_ref[...]
        row = jnp.zeros((heads, TURN), jnp.float32)
        for b in range(table.shape[1]):
            row = jnp.where(bucket_ids == b, values[:, b : b + 1], row)
        for h in range(heads):
            wide = jnp.broadcast_to(row[h : h + 1, :], (PAGE, TURN))
            turned = pltpu.roll(wide, 0, 1, stride=1, stride_axis=0)
            out_ref[h * PAGE : (h + 1) * PAGE, :] = turned[:, :SPREAD]

    return pl.pallas_call(
        body,
        out_shape=jax.ShapeDtypeStruct((heads * PAGE, SPREAD), jnp.float32),
        compiler_params=pltpu.CompilerParams(vmem_limit_bytes=16 * MIB),
        cost_estimate=pl.CostEstimate(flops=0, transcendentals=0, bytes_accessed=48 * MIB),
        name="bias_tiles",
    )(table)


def normalize(side, first_refs, second_refs, gain_ref, out_ref):
    half = first_refs[0].shape[-1]
    for i, (first_ref, second_ref) in enumerate(zip(first_refs, second_refs)):
        first = first_ref[...].astype(jnp.float32)
        second = second_ref[...].astype(jnp.float32)
        total = jnp.sum(first * first, axis=-1, keepdims=True) + jnp.sum(
            second * second, axis=-1, keepdims=True
        )
        scale = lax.rsqrt(total * (1.0 / (2 * half)) + epsilon)
        left = jnp.where(side == 0, first, second)
        right = jnp.where(side == 0, second, first)
        rows = slice(i * PAGE, (i + 1) * PAGE)
        out_ref[rows, :half] = (left * scale * gain_ref[:, :half]).astype(jnp.bfloat16)
        out_ref[rows, half:] = (right * scale * gain_ref[:, half:]).astype(jnp.bfloat16)


def project(part, first, second, side, gain, weights, earlier):
    half = first[0].shape[1]
    columns = weights[0].shape[1]

    starts = range(0, columns, GROUP)

    def body(side_ref, f0, f1, s0, s1, gain_ref, wq, wk, wv, *rest):
        q_out, k_out, v_out, own_out, normed, held, sems = rest[-7:]
        copies = []
        for n, start in enumerate(starts):
            here = slice(start, start + GROUP)
            for i, w_ref in enumerate((wq, wk, wv)):
                copy = pltpu.make_async_copy(w_ref.at[:, here], held.at[i, :, here], sems.at[n, i])
                copy.start()
                copies.append(copy)
        normalize(side_ref[0], (f0, f1), (s0, s1), gain_ref, normed)
        own_out[0] = f0[...]
        own_out[1] = f1[...]
        for n, start in enumerate(starts):
            here = slice(start, start + GROUP)
            for i, out in enumerate((q_out, k_out, v_out)):
                copies[3 * n + i].wait()
                product = jnp.dot(normed[...], held[i, :, here], preferred_element_type=jnp.float32)
                out[:, :, here] = product.astype(jnp.bfloat16).reshape(2, PAGE, GROUP)

    out = pl.BlockSpec((2, PAGE, columns), lambda n, s: (part, 0, 0))
    own = pl.BlockSpec((2, PAGE, half), lambda n, s: (part, 0, 0))
    shape = jax.ShapeDtypeStruct((4, PAGE, columns), jnp.bfloat16)
    return pl.pallas_call(
        body,
        grid_spec=pltpu.PrefetchScalarGridSpec(
            num_scalar_prefetch=1,
            grid=(1,),
            in_specs=[vmem_spec()] * 5 + [hbm_spec()] * 3 + [any_spec()] * len(earlier),
            out_specs=[out, out, out, own],
            scratch_shapes=[
                pltpu.VMEM((2 * PAGE, 2 * half), jnp.bfloat16),
                pltpu.VMEM((3, 2 * half, columns), jnp.bfloat16),
                pltpu.SemaphoreType.DMA((len(starts), 3)),
            ],
        ),
        out_shape=[shape, shape, shape, jax.ShapeDtypeStruct((4, PAGE, half), jnp.bfloat16)],
        input_output_aliases={9 + i: i for i in range(len(earlier))},
        compiler_params=params(24),
        cost_estimate=pl.CostEstimate(
            flops=2 * 2 * PAGE * 2 * half * 3 * columns,
            transcendentals=0,
            bytes_accessed=2 * 2 * half * columns,
        ),
        name="project",
    )(side, *first, *second, gain, *weights, *earlier)


def lane_of(meta, block):
    lane = jnp.int32(0)
    for m in range(1, 4):
        lane = jnp.where(meta[2 * m] == block, m, lane)
    return lane


def attend(lanes, meta, segments, side, queries, keys_local, values_local, w_out, bias):
    inner = w_out.shape[0]
    width = w_out.shape[1]
    pair = 2 * HEAD_DIM
    pairs = inner // pair
    tall = 2 * PAGE

    def body(meta_ref, seg_ref, side_ref, q_ref, k_ref, v_ref, rows_ref, w_ref, bias_ref,
             own_out, send_out, ctx, m_sc, a_sc, seg_sc):
        low = lax.broadcasted_iota(jnp.int32, (PAGE, pair), 1) < HEAD_DIM
        ones = jnp.ones((PAGE, PAGE), jnp.bfloat16)

        def hidden_pairs(i, key_block):
            same = seg_sc[i] == rows_ref[pl.ds(key_block, 1), :]
            return jnp.where(same, 0.0, NEG).astype(jnp.float32)

        def scores(at, key_at, hide, tile, p):
            cols = slice(p * pair, (p + 1) * pair)
            q = q_ref[at, :, cols]
            zero = jnp.zeros_like(q)
            stacked = jnp.concatenate([jnp.where(low, q, zero), jnp.where(low, zero, q)], axis=0)
            s = lax.dot_general(
                stacked, k_ref[key_at, :, cols], (((1,), (1,)), ((), ())),
                preferred_element_type=jnp.float32,
            )
            s = s + bias_ref[p * tall : (p + 1) * tall, tile]
            return s + jnp.concatenate([hide, hide], axis=0)

        def weighted(weights, key_at, p):
            wide = jnp.concatenate([v_ref[key_at, :, p * pair : (p + 1) * pair], ones], axis=1)
            return jnp.dot(weights, wide, preferred_element_type=jnp.float32)

        places = []
        for i, m in enumerate(lanes):
            block = meta_ref[8 + m]
            row = rows_ref[pl.ds(block, 1), :]
            seg_sc[i] = jnp.transpose(jnp.broadcast_to(row, (PAGE, PAGE)))
            places.append((block, lane_of(meta_ref, block)))
        for i, (block, at) in enumerate(places):
            hide = hidden_pairs(i, block)
            for p in range(pairs):
                s = scores(at, at, hide, slice(2 * PAGE, 3 * PAGE), p)
                top = jnp.max(s, axis=-1, keepdims=True)
                weights = jnp.exp(s - top).astype(jnp.bfloat16)
                m_sc[i, p] = jnp.broadcast_to(top, (tall, PAGE))
                a_sc[i, p] = weighted(weights, at, p)

        @pl.loop(0, 8)
        def _(turn):
            i = turn // 4
            slot = turn % 4
            delta = jnp.where(slot < 2, slot - 2, slot - 1)
            block = jnp.where(i == 0, places[0][0], places[1][0])
            at = jnp.where(i == 0, places[0][1], places[1][1])
            key_block = block + delta
            last = jnp.minimum(block, key_block) * PAGE + PAGE - 1
            first = jnp.maximum(block, key_block) * PAGE
            top_index = 4 * PAGE - 1
            joined = seg_ref[jnp.clip(last, 0, top_index)] == seg_ref[jnp.clip(first, 0, top_index)]
            inside = jnp.logical_and(key_block >= 0, key_block < 4)

            @pl.when(jnp.logical_and(inside, joined))
            def _():
                key_at = lane_of(meta_ref, key_block)
                hide = hidden_pairs(i, key_block)
                tile = pl.ds(pl.multiple_of((delta + 2) * PAGE, PAGE), PAGE)
                for p in range(pairs):
                    s = scores(at, key_at, hide, tile, p)
                    before = m_sc[i, p]
                    top = jnp.maximum(before, jnp.max(s, axis=-1, keepdims=True))
                    fade = jnp.exp(before - top)
                    weights = jnp.exp(s - top).astype(jnp.bfloat16)
                    m_sc[i, p] = top
                    a_sc[i, p] = a_sc[i, p] * jnp.concatenate([fade, fade], axis=1) + weighted(
                        weights, key_at, p
                    )

        for i in range(2):
            for p in range(pairs):
                mixed = jnp.where(low, a_sc[i, p, :PAGE, :pair], a_sc[i, p, PAGE:, :pair])
                total = jnp.where(low, a_sc[i, p, :PAGE, pair:], a_sc[i, p, PAGE:, pair:])
                ctx[i * PAGE : (i + 1) * PAGE, p * pair : (p + 1) * pair] = (mixed / total).astype(
                    jnp.bfloat16
                )

        half = width // 2
        for out, here in ((own_out, side_ref[0]), (send_out, 1 - side_ref[0])):
            for start in range(0, half, GROUP):
                at = pl.multiple_of(here * half + start, GROUP)
                out[:, start : start + GROUP] = jnp.dot(
                    ctx[...], w_ref[:, pl.ds(at, GROUP)], preferred_element_type=jnp.float32
                ).astype(jnp.bfloat16)

    shape = jax.ShapeDtypeStruct((tall, width // 2), jnp.bfloat16)
    return pl.pallas_call(
        body,
        grid_spec=pltpu.PrefetchScalarGridSpec(
            num_scalar_prefetch=3,
            grid=(1,),
            in_specs=[vmem_spec()] * 6,
            out_specs=[vmem_spec()] * 2,
            scratch_shapes=[
                pltpu.VMEM((tall, inner), jnp.bfloat16),
                pltpu.VMEM((2, pairs, tall, PAGE), jnp.float32),
                pltpu.VMEM((2, pairs, tall, pair + PAGE), jnp.float32),
                pltpu.VMEM((2, PAGE, PAGE), jnp.int32),
            ],
        ),
        out_shape=[shape, shape],
        compiler_params=params(24),
        cost_estimate=pl.CostEstimate(
            flops=2 * tall * inner * width * 2,
            transcendentals=tall * 512 * 16,
            bytes_accessed=10 * MIB,
        ),
        name="attend",
    )(meta, segments, side, queries, keys_local, values_local,
      segments.reshape(4, PAGE), w_out, bias)


def residual(lanes, meta, own, received, packed, earlier):
    half = own.shape[1]

    def page(i, meta_ref):
        return jnp.where(i == 0, meta_ref[8 + lanes[0]], meta_ref[8 + lanes[1]])

    def body(meta_ref, own_ref, got_ref, packed_ref, *rest):
        out, first, second = rest[-3:]
        added = own_ref[...].astype(jnp.float32) + got_ref[...].astype(jnp.float32)
        value = (packed_ref[0].astype(jnp.float32) + added).astype(jnp.bfloat16)
        out[0] = value

        @pl.when(pl.program_id(0) == 0)
        def _():
            first[...] = value

        @pl.when(pl.program_id(0) == 1)
        def _():
            second[...] = value

    block = pl.BlockSpec((PAGE, half), lambda i, s: (i, 0))
    alone = pl.BlockSpec((PAGE, half), lambda i, s: (0, 0))
    shape = jax.ShapeDtypeStruct((PAGE, half), jnp.bfloat16)
    return pl.pallas_call(
        body,
        grid_spec=pltpu.PrefetchScalarGridSpec(
            num_scalar_prefetch=1,
            grid=(2,),
            in_specs=[
                block,
                block,
                pl.BlockSpec((1, PAGE, half), lambda i, s: (lane_of(s, page(i, s)), 0, 0)),
            ]
            + [any_spec()] * len(earlier),
            out_specs=[pl.BlockSpec((1, PAGE, half), lambda i, s: (page(i, s), 0, 0)), alone, alone],
        ),
        out_shape=[jax.ShapeDtypeStruct((4, PAGE, half), jnp.bfloat16), shape, shape],
        input_output_aliases={4 + i: i for i in range(len(earlier))},
        compiler_params=params(8),
        name="residual",
    )(meta, own, received, packed, *earlier)


def cross(lanes, meta, side, first, second, gain, cross_key, cross_value, earlier):
    half = first[0].shape[1]
    columns = cross_key.shape[1]

    def body(meta_ref, side_ref, f0, f1, s0, s1, gain_ref, wk, wv, *rest):
        out, final, pages, sems = rest[-4:]
        normalize(side_ref[0], (f0, f1), (s0, s1), gain_ref, final)
        copies = []
        for start in range(0, columns, GROUP):
            here = slice(start, start + GROUP)
            keys_part, values_part = (
                jnp.dot(final[...], w_ref[:, here], preferred_element_type=jnp.float32).astype(jnp.bfloat16)
                for w_ref in (wk, wv)
            )
            both = jnp.stack([keys_part, values_part], axis=1)
            for i, m in enumerate(lanes):
                pages[i, :, :, here] = both[i * PAGE : (i + 1) * PAGE]
        for i, m in enumerate(lanes):
            copy = pltpu.make_async_copy(pages.at[i], out.at[meta_ref[2 * m + 1]], sems.at[i])
            copy.start()
            copies.append(copy)
        for copy in copies:
            copy.wait()

    return pl.pallas_call(
        body,
        grid_spec=pltpu.PrefetchScalarGridSpec(
            num_scalar_prefetch=2,
            grid=(1,),
            in_specs=[vmem_spec()] * 7 + [any_spec()] * len(earlier),
            out_specs=any_spec(),
            scratch_shapes=[
                pltpu.VMEM((2 * PAGE, 2 * half), jnp.bfloat16),
                pltpu.VMEM((2, PAGE, 2, columns), jnp.bfloat16),
                pltpu.SemaphoreType.DMA((2,)),
            ],
        ),
        out_shape=jax.ShapeDtypeStruct((4, PAGE, 2, columns), jnp.bfloat16),
        input_output_aliases={9: 0} if earlier else {},
        compiler_params=params(24),
        cost_estimate=pl.CostEstimate(
            flops=2 * 2 * PAGE * 2 * half * 2 * columns,
            transcendentals=0,
            bytes_accessed=2 * 2 * half * columns * 2,
        ),
        name="cross",
    )(meta, side, *first, *second, gain, cross_key, cross_value, *earlier)


def near(rows):
    other_zero = exchange(rows[0], 0, 1)
    own_one = exchange(rows[1], 1, 0)
    other_one = exchange(rows[1], 1, 1)
    return (rows[0], own_one), (other_zero, other_one)


def far(rows):
    other_two = exchange(rows[0], 2, 1)
    other_three = exchange(rows[1], 3, 1)
    own_two = exchange(other_two, 0, 1)
    own_three = exchange(other_three, 0, 1)
    return (own_two, own_three), (other_two, other_three)


def shards(
    arrivals,
    packing,
    segment_ids,
    page_table,
    attn_gain,
    w_query,
    w_key,
    w_value,
    w_out,
    rel_bias,
    final_gain,
    cross_key,
    cross_value,
):
    token_count, half = arrivals.shape
    me = lax.axis_index("req").astype(jnp.int32).reshape(1)
    side = lax.axis_index("tp").astype(jnp.int32).reshape(1)
    rows, tags, pages = lane_order(packing, page_table, arrivals.reshape(4, PAGE, half), me)
    far_own, far_other = far(rows[2:])
    near_own, near_other = near(rows[:2])
    meta = jnp.concatenate([tags[0]] + [exchange(tags[m], m, 0) for m in (1, 2, 3)] + [pages])
    bias = bias_tiles(rel_bias)
    attn_row = attn_gain.reshape(1, 2 * half)
    final_row = final_gain.reshape(1, 2 * half)
    weights = tuple(
        pltpu.with_memory_space_constraint(w, pltpu.HBM) for w in (w_query, w_key, w_value)
    )
    held = project(0, near_own, near_other, side, attn_row, weights, ())
    queries, keys_local, values_local, packed = project(
        1, far_own, far_other, side, attn_row, weights, tuple(held)
    )
    own_far, send_far = attend(
        (2, 3), meta, segment_ids, side, queries, keys_local, values_local, w_out, bias
    )
    got_far = exchange(send_far, 0, 1)
    own_near, send_near = attend(
        (0, 1), meta, segment_ids, side, queries, keys_local, values_local, w_out, bias
    )
    got_near = exchange(send_near, 0, 1)
    hidden, hidden_two, hidden_three = residual((2, 3), meta, own_far, got_far, packed, ())
    far_first, far_second = far((hidden_two, hidden_three))
    hidden, hidden_zero, hidden_one = residual((0, 1), meta, own_near, got_near, packed, (hidden,))
    near_first, near_second = near((hidden_zero, hidden_one))
    cache = cross(
        (0, 1), meta, side, near_first, near_second, final_row, cross_key, cross_value, ()
    )
    cache = cross(
        (2, 3), meta, side, far_first, far_second, final_row, cross_key, cross_value, (cache,)
    )
    return (hidden.reshape(token_count, half), cache)


def solution(mesh):
    return jax.shard_map(
        shards,
        mesh=mesh,
        in_specs=(
            P("req", "tp"),
            P("req"),
            P("req"),
            P("req"),
            P(),
            P(None, "tp"),
            P(None, "tp"),
            P(None, "tp"),
            P("tp", None),
            P(None, "tp"),
            P(),
            P(None, "tp"),
            P(None, "tp"),
        ),
        out_specs=(P("req", "tp"), P("req", None, None, "tp")),
        check_vma=False,
    )
```

```python
import jax
import jax.numpy as jnp
from jax import lax
from jax.experimental import pallas as pl
from jax.experimental.pallas import tpu as pltpu
from jax.sharding import PartitionSpec as P

PAGE = 128
HEAD_DIM = 64
SPREAD = 640
TURN = 1024
GROUP = 256
MIB = 1 << 20

epsilon = 1e-06
far_steps = (12, 16, 23, 32, 46, 64, 91)
NEG = float("-inf")


def exchange(block, mask, flip):
    count = lax.axis_size("req")
    pairs = [(r * 2 + t, (r ^ mask) * 2 + (t ^ flip)) for r in range(count) for t in range(2)]
    return lax.ppermute(block, ("req", "tp"), pairs)


def buckets(offsets):
    distance = jnp.abs(offsets)
    far_bucket = 8 + sum((distance >= threshold).astype(jnp.int32) for threshold in far_steps)
    bucket_ids = jnp.where(distance < 8, distance, far_bucket)
    return bucket_ids + jnp.where(offsets > 0, 16, 0).astype(jnp.int32)


def any_spec():
    return pl.BlockSpec(memory_space=pl.ANY)


def smem_spec():
    return pl.BlockSpec(memory_space=pltpu.SMEM)


def hbm_spec():
    return pl.BlockSpec(memory_space=pltpu.HBM)


def vmem_spec():
    return pl.BlockSpec(memory_space=pltpu.VMEM)


def params(mib, grid_rank=1):
    return pltpu.CompilerParams(
        dimension_semantics=("arbitrary",) * grid_rank, vmem_limit_bytes=mib * MIB
    )


def lane_order(packing, page_table, arrived, me):
    def body(packing_ref, table_ref, me_ref, rows_ref, *rest):
        row_outs, tag_outs, page_out = rest[:4], rest[4:8], rest[8]
        me_here = me_ref[0]
        for m in range(4):
            source = jnp.int32(0)
            pack_slot = jnp.int32(0)
            page = jnp.int32(0)
            page_slot = jnp.int32(0)
            for j in range(4):
                hit = ((packing_ref[j] // 4) ^ me_here) == m
                source = jnp.where(hit, j, source)
                pack_slot = jnp.where(hit, packing_ref[j] % 4, pack_slot)
                owned = ((table_ref[j] // 4) ^ me_here) == m
                page = jnp.where(owned, j, page)
                page_slot = jnp.where(owned, table_ref[j] % 4, page_slot)
            tag_outs[m][0] = pack_slot
            tag_outs[m][1] = page_slot
            page_out[m] = page
            row_outs[m][...] = rows_ref[source]

    shape = jax.ShapeDtypeStruct(arrived.shape[1:], arrived.dtype)
    outs = pl.pallas_call(
        body,
        grid_spec=pltpu.PrefetchScalarGridSpec(
            num_scalar_prefetch=3,
            grid=(),
            in_specs=[vmem_spec()],
            out_specs=[vmem_spec()] * 4 + [smem_spec()] * 5,
        ),
        out_shape=[shape] * 4
        + [jax.ShapeDtypeStruct((2,), jnp.int32)] * 4
        + [jax.ShapeDtypeStruct((4,), jnp.int32)],
        compiler_params=pltpu.CompilerParams(vmem_limit_bytes=8 * MIB),
        name="lane_order",
    )(packing, page_table, me, arrived)
    return outs[:4], outs[4:8], outs[8]


def bias_tiles(rel_bias):
    table = jnp.transpose(rel_bias)
    heads = table.shape[0]

    def body(table_ref, out_ref):
        lane = lax.broadcasted_iota(jnp.int32, (heads, TURN), 1)
        bucket_ids = buckets(jnp.where(lane < SPREAD, lane - 2 * PAGE, lane - 2 * PAGE - TURN))
        values = table_ref[...]
        row = jnp.zeros((heads, TURN), jnp.float32)
        for b in range(table.shape[1]):
            row = jnp.where(bucket_ids == b, values[:, b : b + 1], row)
        for h in range(heads):
            wide = jnp.broadcast_to(row[h : h + 1, :], (PAGE, TURN))
            turned = pltpu.roll(wide, 0, 1, stride=1, stride_axis=0)
            out_ref[h * PAGE : (h + 1) * PAGE, :] = turned[:, :SPREAD]

    return pl.pallas_call(
        body,
        out_shape=jax.ShapeDtypeStruct((heads * PAGE, SPREAD), jnp.float32),
        compiler_params=pltpu.CompilerParams(vmem_limit_bytes=16 * MIB),
        cost_estimate=pl.CostEstimate(flops=0, transcendentals=0, bytes_accessed=48 * MIB),
        name="bias_tiles",
    )(table)


def normalize(side, first_refs, second_refs, gain_ref, out_ref):
    half = first_refs[0].shape[-1]
    for i, (first_ref, second_ref) in enumerate(zip(first_refs, second_refs)):
        first = first_ref[...].astype(jnp.float32)
        second = second_ref[...].astype(jnp.float32)
        total = jnp.sum(first * first, axis=-1, keepdims=True) + jnp.sum(
            second * second, axis=-1, keepdims=True
        )
        scale = lax.rsqrt(total * (1.0 / (2 * half)) + epsilon)
        left = jnp.where(side == 0, first, second)
        right = jnp.where(side == 0, second, first)
        rows = slice(i * PAGE, (i + 1) * PAGE)
        out_ref[rows, :half] = (left * scale * gain_ref[:, :half]).astype(jnp.bfloat16)
        out_ref[rows, half:] = (right * scale * gain_ref[:, half:]).astype(jnp.bfloat16)


def project(part, first, second, side, gain, weights, earlier):
    half = first[0].shape[1]
    columns = weights[0].shape[1]

    starts = range(0, columns, GROUP)

    def body(side_ref, f0, f1, s0, s1, gain_ref, wq, wk, wv, *rest):
        q_out, k_out, v_out, own_out, normed, held, sems = rest[-7:]
        copies = []
        for i, w_ref in enumerate((wq, wk, wv)):
            copy = pltpu.make_async_copy(w_ref, held.at[i], sems.at[i])
            copy.start()
            copies.append(copy)
        normalize(side_ref[0], (f0, f1), (s0, s1), gain_ref, normed)
        own_out[0] = f0[...]
        own_out[1] = f1[...]
        for i, out in enumerate((q_out, k_out, v_out)):
            copies[i].wait()
            for start in starts:
                here = slice(start, start + GROUP)
                product = jnp.dot(normed[...], held[i, :, here], preferred_element_type=jnp.float32)
                out[:, :, here] = product.astype(jnp.bfloat16).reshape(2, PAGE, GROUP)

    out = pl.BlockSpec((2, PAGE, columns), lambda n, s: (part, 0, 0))
    own = pl.BlockSpec((2, PAGE, half), lambda n, s: (part, 0, 0))
    shape = jax.ShapeDtypeStruct((4, PAGE, columns), jnp.bfloat16)
    return pl.pallas_call(
        body,
        grid_spec=pltpu.PrefetchScalarGridSpec(
            num_scalar_prefetch=1,
            grid=(1,),
            in_specs=[vmem_spec()] * 5 + [hbm_spec()] * 3 + [any_spec()] * len(earlier),
            out_specs=[out, out, out, own],
            scratch_shapes=[
                pltpu.VMEM((2 * PAGE, 2 * half), jnp.bfloat16),
                pltpu.VMEM((3, 2 * half, columns), jnp.bfloat16),
                pltpu.SemaphoreType.DMA((3,)),
            ],
        ),
        out_shape=[shape, shape, shape, jax.ShapeDtypeStruct((4, PAGE, half), jnp.bfloat16)],
        input_output_aliases={9 + i: i for i in range(len(earlier))},
        compiler_params=params(24),
        cost_estimate=pl.CostEstimate(
            flops=2 * 2 * PAGE * 2 * half * 3 * columns,
            transcendentals=0,
            bytes_accessed=2 * 2 * half * columns,
        ),
        name="project",
    )(side, *first, *second, gain, *weights, *earlier)


def lane_of(meta, block):
    lane = jnp.int32(0)
    for m in range(1, 4):
        lane = jnp.where(meta[2 * m] == block, m, lane)
    return lane


def attend(lanes, meta, segments, side, queries, keys_local, values_local, w_out, bias):
    inner = w_out.shape[0]
    width = w_out.shape[1]
    pair = 2 * HEAD_DIM
    pairs = inner // pair
    tall = 2 * PAGE

    def body(meta_ref, seg_ref, side_ref, q_ref, k_ref, v_ref, rows_ref, w_ref, bias_ref,
             own_out, send_out, ctx, m_sc, a_sc, seg_sc):
        low = lax.broadcasted_iota(jnp.int32, (PAGE, pair), 1) < HEAD_DIM
        ones = jnp.ones((PAGE, PAGE), jnp.bfloat16)

        def hidden_pairs(i, key_block):
            same = seg_sc[i] == rows_ref[pl.ds(key_block, 1), :]
            return jnp.where(same, 0.0, NEG).astype(jnp.float32)

        def scores(at, key_at, hide, tile, p):
            cols = slice(p * pair, (p + 1) * pair)
            q = q_ref[at, :, cols]
            zero = jnp.zeros_like(q)
            stacked = jnp.concatenate([jnp.where(low, q, zero), jnp.where(low, zero, q)], axis=0)
            s = lax.dot_general(
                stacked, k_ref[key_at, :, cols], (((1,), (1,)), ((), ())),
                preferred_element_type=jnp.float32,
            )
            s = s + bias_ref[p * tall : (p + 1) * tall, tile]
            return s + jnp.concatenate([hide, hide], axis=0)

        def weighted(weights, key_at, p):
            wide = jnp.concatenate([v_ref[key_at, :, p * pair : (p + 1) * pair], ones], axis=1)
            return jnp.dot(weights, wide, preferred_element_type=jnp.float32)

        places = []
        for i, m in enumerate(lanes):
            block = meta_ref[8 + m]
            row = rows_ref[pl.ds(block, 1), :]
            seg_sc[i] = jnp.transpose(jnp.broadcast_to(row, (PAGE, PAGE)))
            places.append((block, lane_of(meta_ref, block)))
        for i, (block, at) in enumerate(places):
            hide = hidden_pairs(i, block)
            for p in range(pairs):
                s = scores(at, at, hide, slice(2 * PAGE, 3 * PAGE), p)
                top = jnp.max(s, axis=-1, keepdims=True)
                weights = jnp.exp(s - top).astype(jnp.bfloat16)
                m_sc[i, p] = jnp.broadcast_to(top, (tall, PAGE))
                a_sc[i, p] = weighted(weights, at, p)

        @pl.loop(0, 8)
        def _(turn):
            i = turn // 4
            slot = turn % 4
            delta = jnp.where(slot < 2, slot - 2, slot - 1)
            block = jnp.where(i == 0, places[0][0], places[1][0])
            at = jnp.where(i == 0, places[0][1], places[1][1])
            key_block = block + delta
            last = jnp.minimum(block, key_block) * PAGE + PAGE - 1
            first = jnp.maximum(block, key_block) * PAGE
            top_index = 4 * PAGE - 1
            joined = seg_ref[jnp.clip(last, 0, top_index)] == seg_ref[jnp.clip(first, 0, top_index)]
            inside = jnp.logical_and(key_block >= 0, key_block < 4)

            @pl.when(jnp.logical_and(inside, joined))
            def _():
                key_at = lane_of(meta_ref, key_block)
                hide = hidden_pairs(i, key_block)
                tile = pl.ds(pl.multiple_of((delta + 2) * PAGE, PAGE), PAGE)
                for p in range(pairs):
                    s = scores(at, key_at, hide, tile, p)
                    before = m_sc[i, p]
                    top = jnp.maximum(before, jnp.max(s, axis=-1, keepdims=True))
                    fade = jnp.exp(before - top)
                    weights = jnp.exp(s - top).astype(jnp.bfloat16)
                    m_sc[i, p] = top
                    a_sc[i, p] = a_sc[i, p] * jnp.concatenate([fade, fade], axis=1) + weighted(
                        weights, key_at, p
                    )

        for i in range(2):
            for p in range(pairs):
                mixed = jnp.where(low, a_sc[i, p, :PAGE, :pair], a_sc[i, p, PAGE:, :pair])
                total = jnp.where(low, a_sc[i, p, :PAGE, pair:], a_sc[i, p, PAGE:, pair:])
                ctx[i * PAGE : (i + 1) * PAGE, p * pair : (p + 1) * pair] = (mixed / total).astype(
                    jnp.bfloat16
                )

        half = width // 2
        for out, here in ((own_out, side_ref[0]), (send_out, 1 - side_ref[0])):
            for start in range(0, half, GROUP):
                at = pl.multiple_of(here * half + start, GROUP)
                out[:, start : start + GROUP] = jnp.dot(
                    ctx[...], w_ref[:, pl.ds(at, GROUP)], preferred_element_type=jnp.float32
                ).astype(jnp.bfloat16)

    shape = jax.ShapeDtypeStruct((tall, width // 2), jnp.bfloat16)
    return pl.pallas_call(
        body,
        grid_spec=pltpu.PrefetchScalarGridSpec(
            num_scalar_prefetch=3,
            grid=(1,),
            in_specs=[vmem_spec()] * 6,
            out_specs=[vmem_spec()] * 2,
            scratch_shapes=[
                pltpu.VMEM((tall, inner), jnp.bfloat16),
                pltpu.VMEM((2, pairs, tall, PAGE), jnp.float32),
                pltpu.VMEM((2, pairs, tall, pair + PAGE), jnp.float32),
                pltpu.VMEM((2, PAGE, PAGE), jnp.int32),
            ],
        ),
        out_shape=[shape, shape],
        compiler_params=params(24),
        cost_estimate=pl.CostEstimate(
            flops=2 * tall * inner * width * 2,
            transcendentals=tall * 512 * 16,
            bytes_accessed=10 * MIB,
        ),
        name="attend",
    )(meta, segments, side, queries, keys_local, values_local,
      segments.reshape(4, PAGE), w_out, bias)


def residual(lanes, meta, own, received, packed, earlier):
    half = own.shape[1]

    def page(i, meta_ref):
        return jnp.where(i == 0, meta_ref[8 + lanes[0]], meta_ref[8 + lanes[1]])

    def body(meta_ref, own_ref, got_ref, packed_ref, *rest):
        out, first, second = rest[-3:]
        added = own_ref[...].astype(jnp.float32) + got_ref[...].astype(jnp.float32)
        value = (packed_ref[0].astype(jnp.float32) + added).astype(jnp.bfloat16)
        out[0] = value

        @pl.when(pl.program_id(0) == 0)
        def _():
            first[...] = value

        @pl.when(pl.program_id(0) == 1)
        def _():
            second[...] = value

    block = pl.BlockSpec((PAGE, half), lambda i, s: (i, 0))
    alone = pl.BlockSpec((PAGE, half), lambda i, s: (0, 0))
    shape = jax.ShapeDtypeStruct((PAGE, half), jnp.bfloat16)
    return pl.pallas_call(
        body,
        grid_spec=pltpu.PrefetchScalarGridSpec(
            num_scalar_prefetch=1,
            grid=(2,),
            in_specs=[
                block,
                block,
                pl.BlockSpec((1, PAGE, half), lambda i, s: (lane_of(s, page(i, s)), 0, 0)),
            ]
            + [any_spec()] * len(earlier),
            out_specs=[pl.BlockSpec((1, PAGE, half), lambda i, s: (page(i, s), 0, 0)), alone, alone],
        ),
        out_shape=[jax.ShapeDtypeStruct((4, PAGE, half), jnp.bfloat16), shape, shape],
        input_output_aliases={4 + i: i for i in range(len(earlier))},
        compiler_params=params(8),
        name="residual",
    )(meta, own, received, packed, *earlier)


def cross(lanes, meta, side, first, second, gain, cross_key, cross_value, earlier):
    half = first[0].shape[1]
    columns = cross_key.shape[1]

    def body(meta_ref, side_ref, f0, f1, s0, s1, gain_ref, wk, wv, *rest):
        out, final, pages, sems = rest[-4:]
        normalize(side_ref[0], (f0, f1), (s0, s1), gain_ref, final)
        copies = []
        for start in range(0, columns, GROUP):
            here = slice(start, start + GROUP)
            keys_part, values_part = (
                jnp.dot(final[...], w_ref[:, here], preferred_element_type=jnp.float32).astype(jnp.bfloat16)
                for w_ref in (wk, wv)
            )
            both = jnp.stack([keys_part, values_part], axis=1)
            for i, m in enumerate(lanes):
                pages[i, :, :, here] = both[i * PAGE : (i + 1) * PAGE]
        for i, m in enumerate(lanes):
            copy = pltpu.make_async_copy(pages.at[i], out.at[meta_ref[2 * m + 1]], sems.at[i])
            copy.start()
            copies.append(copy)
        for copy in copies:
            copy.wait()

    return pl.pallas_call(
        body,
        grid_spec=pltpu.PrefetchScalarGridSpec(
            num_scalar_prefetch=2,
            grid=(1,),
            in_specs=[vmem_spec()] * 7 + [any_spec()] * len(earlier),
            out_specs=any_spec(),
            scratch_shapes=[
                pltpu.VMEM((2 * PAGE, 2 * half), jnp.bfloat16),
                pltpu.VMEM((2, PAGE, 2, columns), jnp.bfloat16),
                pltpu.SemaphoreType.DMA((2,)),
            ],
        ),
        out_shape=jax.ShapeDtypeStruct((4, PAGE, 2, columns), jnp.bfloat16),
        input_output_aliases={9: 0} if earlier else {},
        compiler_params=params(24),
        cost_estimate=pl.CostEstimate(
            flops=2 * 2 * PAGE * 2 * half * 2 * columns,
            transcendentals=0,
            bytes_accessed=2 * 2 * half * columns * 2,
        ),
        name="cross",
    )(meta, side, *first, *second, gain, cross_key, cross_value, *earlier)


def near(rows):
    other_zero = exchange(rows[0], 0, 1)
    own_one = exchange(rows[1], 1, 0)
    other_one = exchange(rows[1], 1, 1)
    return (rows[0], own_one), (other_zero, other_one)


def far(rows):
    other_two = exchange(rows[0], 2, 1)
    other_three = exchange(rows[1], 3, 1)
    own_two = exchange(other_two, 0, 1)
    own_three = exchange(other_three, 0, 1)
    return (own_two, own_three), (other_two, other_three)


def shards(
    arrivals,
    packing,
    segment_ids,
    page_table,
    attn_gain,
    w_query,
    w_key,
    w_value,
    w_out,
    rel_bias,
    final_gain,
    cross_key,
    cross_value,
):
    token_count, half = arrivals.shape
    me = lax.axis_index("req").astype(jnp.int32).reshape(1)
    side = lax.axis_index("tp").astype(jnp.int32).reshape(1)
    rows, tags, pages = lane_order(packing, page_table, arrivals.reshape(4, PAGE, half), me)
    far_own, far_other = far(rows[2:])
    near_own, near_other = near(rows[:2])
    meta = jnp.concatenate([tags[0]] + [exchange(tags[m], m, 0) for m in (1, 2, 3)] + [pages])
    bias = bias_tiles(rel_bias)
    attn_row = attn_gain.reshape(1, 2 * half)
    final_row = final_gain.reshape(1, 2 * half)
    weights = tuple(
        pltpu.with_memory_space_constraint(w, pltpu.HBM) for w in (w_query, w_key, w_value)
    )
    held = project(0, near_own, near_other, side, attn_row, weights, ())
    queries, keys_local, values_local, packed = project(
        1, far_own, far_other, side, attn_row, weights, tuple(held)
    )
    own_far, send_far = attend(
        (2, 3), meta, segment_ids, side, queries, keys_local, values_local, w_out, bias
    )
    got_far = exchange(send_far, 0, 1)
    own_near, send_near = attend(
        (0, 1), meta, segment_ids, side, queries, keys_local, values_local, w_out, bias
    )
    got_near = exchange(send_near, 0, 1)
    hidden, hidden_two, hidden_three = residual((2, 3), meta, own_far, got_far, packed, ())
    far_first, far_second = far((hidden_two, hidden_three))
    hidden, hidden_zero, hidden_one = residual((0, 1), meta, own_near, got_near, packed, (hidden,))
    near_first, near_second = near((hidden_zero, hidden_one))
    cache = cross(
        (0, 1), meta, side, near_first, near_second, final_row, cross_key, cross_value, ()
    )
    cache = cross(
        (2, 3), meta, side, far_first, far_second, final_row, cross_key, cross_value, (cache,)
    )
    return (hidden.reshape(token_count, half), cache)


def solution(mesh):
    return jax.shard_map(
        shards,
        mesh=mesh,
        in_specs=(
            P("req", "tp"),
            P("req"),
            P("req"),
            P("req"),
            P(),
            P(None, "tp"),
            P(None, "tp"),
            P(None, "tp"),
            P("tp", None),
            P(None, "tp"),
            P(),
            P(None, "tp"),
            P(None, "tp"),
        ),
        out_specs=(P("req", "tp"), P("req", None, None, "tp")),
        check_vma=False,
    )
```
